32 devices in a mesh: grp: 2 (over x), tm: 16 (over z, y, core).
Axes of the slice: x: 2, y: 2, z: 4, core: 2. Of those that a mesh axis runs over, the one named last changes fastest.
Arguments:
- frames_in: bfloat16 [16384, 1536], P(('grp', 'tm')), parts along dimension 0, may hold values from -6 to 6
- frame_time: int32 [64], P('grp'), parts along dimension 0, may hold values from 0 to 31, each once
- norm_gain: float32 [1536], replicated, may hold values from 0.25 to 1.75
- w_query: bfloat16 [1536, 768], replicated, may hold values from -2 to 2
- w_key: bfloat16 [1536, 768], replicated, may hold values from -2 to 2
- w_value: bfloat16 [1536, 768], replicated, may hold values from -0.15625 to 0.15625
- w_output: bfloat16 [768, 1536], replicated, may hold values from -0.21875 to 0.21875
Outputs:
- attended: bfloat16 [16384, 1536], P(('grp', 'tm')), parts along dimension 0
The draws below stay inside these ranges and needn't reach their ends.
There are 2 independent parts, one for each index of `grp`. The reference program is written for one: setup_inputs(seed, part) draws one part's arguments, and reference() takes and returns one part's arrays. A program takes and returns all parts, laid end to end along the dimension named above; an argument that names none is the same for every part. Nothing has to cross between parts.
Inputs may be any that keep to these rules, and one draw needn't show every extreme that they name: `frame_time`: each of 0 to 31 stands once.
All inputs are finite; a program needn't handle non-finite values.
Results may differ from the reference program's by a relative error of at most 0.004.
The reference program's roundings to bfloat16 on the way count: a program that leaves them out, or rounds other values in their place, can miss the bound.
Values may be sent and summed in bfloat16 or wider, within the bound.
A program may use at most 128 MiB of HBM per device.

```python
import jax
import jax.numpy as jnp
from jax import lax

D = 1536
HEADS = 6
HD = 128
HH = 16
WW = 16
WIN = 8
POOL = 4
FRAMES = 32
PK = 16


def projection(key, salt):
    base = jnp.clip(jax.random.normal(jax.random.fold_in(key, salt), (D, HEADS * HD), jnp.float32), -6.0, 6.0) * D ** (-0.5)
    return jnp.clip(base, -2.0, 2.0)


def draw_w_query(key, part):
    return projection(key, 1).astype(jnp.bfloat16)


def draw_w_key(key, part):
    return projection(key, 2).astype(jnp.bfloat16)


def shard_levels(key, extent, split, smallest, top_value):
    def one(position, parts):
        steps = jax.random.uniform(jax.random.fold_in(jax.random.fold_in(key, 6), position), (parts,), jnp.float32, smallest / len(split), top_value / len(split))
        return jnp.repeat(jnp.exp(steps), extent[position] // parts).reshape((-1,) + (1,) * (len(extent) - position - 1))

    factor_of = one(*split[0])
    for cut in split[1:]:
        factor_of = factor_of * one(*cut)
    return factor_of


def normal_values(key, shape, deviation, reach, cuts=(), kind=jnp.bfloat16):
    result = jax.random.normal(key, shape, jnp.float32) * deviation
    if len(cuts) > 0:
        result = shard_levels(key, shape, cuts, -0.22, 0.18) * result
    return jnp.clip(result, min=-reach, max=reach).astype(kind)


def setup_inputs(seed: int = 0, part: int = 0) -> dict:
    key_of = jax.random.split(jax.random.key(seed), 8)
    part_keys = jax.random.split(jax.random.fold_in(key_of[7], part), 8)
    frames_in = normal_values(part_keys[0], (FRAMES * HH * WW, D), 1.0, 6.0, ((0, 16),))
    frame_time = jax.random.permutation(part_keys[1], FRAMES).astype(jnp.int32)
    norm_gain = jnp.clip(1.0 + 0.15 * jax.random.normal(key_of[2], (D,), jnp.float32), 0.25, 1.75)
    w_query = draw_w_query(jax.random.fold_in(key_of[7], 71), part)
    w_key = draw_w_key(jax.random.fold_in(key_of[7], 71), part)
    w_value = normal_values(key_of[5], (D, HEADS * HD), D ** -0.5, 0.15625)
    w_output = normal_values(key_of[6], (HEADS * HD, D), (HEADS * HD) ** -0.5, 0.21875)
    return {"frames_in": frames_in, "frame_time": frame_time, "norm_gain": norm_gain, "w_query": w_query, "w_key": w_key, "w_value": w_value, "w_output": w_output}


def normed_rows(frames_in, norm_gain):
    values_f = frames_in.astype(jnp.float32)
    scale = lax.rsqrt(lax.optimization_barrier(jnp.mean(values_f * values_f, axis=-1, keepdims=True)) + 1e-06)
    return (values_f * scale * norm_gain.astype(jnp.float32)).astype(jnp.bfloat16)

def to_windows(array, count):
    shaped = array.reshape(count, HH // WIN, WIN, WW // WIN, WIN, HEADS, HD)
    shaped = shaped.transpose(0, 1, 3, 2, 4, 5, 6)
    return shaped.reshape(count, HH // WIN * (WW // WIN), WIN * WIN, HEADS, HD)

def from_windows(array, count):
    shaped = array.reshape(count, HH // WIN, WW // WIN, WIN, WIN, HEADS * HD)
    shaped = shaped.transpose(0, 1, 3, 2, 4, 5)
    return shaped.reshape(count * HH * WW, HEADS * HD)

def pooled(array, count):
    shaped = array.reshape(count, HH // POOL, POOL, WW // POOL, POOL, HEADS * HD).astype(jnp.float32)
    return lax.optimization_barrier(jnp.mean(shaped, axis=(2, 4))).reshape(count * PK, HEADS, HD).astype(jnp.bfloat16)

def reference(frames_in, frame_time, norm_gain, w_query, w_key, w_value, w_output):
    count = frame_time.shape[0]
    normed = normed_rows(frames_in, norm_gain)
    query = jnp.dot(normed, w_query, preferred_element_type=jnp.float32).astype(jnp.bfloat16)
    keys = jnp.dot(normed, w_key, preferred_element_type=jnp.float32).astype(jnp.bfloat16)
    values = jnp.dot(normed, w_value, preferred_element_type=jnp.float32).astype(jnp.bfloat16)
    pooled_keys = lax.optimization_barrier(pooled(keys, count)).astype(jnp.float32)
    pooled_values = lax.optimization_barrier(pooled(values, count)).astype(jnp.float32)
    key_time = jnp.repeat(frame_time, PK)
    query_win = to_windows(query, count)
    keys_win = to_windows(keys, count)
    values_win = to_windows(values, count)
    factor = 1.0 / HD ** 0.5

    def one_frame(items):
        q_frame, k_frame, v_frame, t_frame = items
        q32 = q_frame.astype(jnp.float32)
        local_s = jnp.einsum('nqhd,nkhd->nhqk', q32, k_frame.astype(jnp.float32)) * factor
        far_s = jnp.einsum('nqhd,khd->nhqk', q32, pooled_keys) * factor
        valid = key_time < t_frame
        far_s = jnp.where(valid, far_s, -1e+30)
        top = jnp.maximum(lax.optimization_barrier(jnp.max(local_s, -1)), lax.optimization_barrier(jnp.max(far_s, -1)))
        local_w = jnp.exp(local_s - top[..., None])
        far_w = jnp.where(valid, jnp.exp(far_s - top[..., None]), 0.0)
        total = lax.optimization_barrier(jnp.sum(local_w, -1)) + lax.optimization_barrier(jnp.sum(far_w, -1))
        local_p = lax.optimization_barrier(local_w.astype(jnp.bfloat16)).astype(jnp.float32)
        far_p = lax.optimization_barrier(far_w.astype(jnp.bfloat16)).astype(jnp.float32)
        acc = jnp.einsum('nhqk,nkhd->nhqd', local_p, v_frame.astype(jnp.float32))
        acc = acc + jnp.einsum('nhqk,khd->nhqd', far_p, pooled_values)
        mixed = acc / total[..., None]
        return mixed.transpose(0, 2, 1, 3).astype(jnp.bfloat16)
    mixed = lax.map(one_frame, (query_win, keys_win, values_win, frame_time))
    mixed = from_windows(mixed, count)
    return jnp.dot(mixed, w_output, preferred_element_type=jnp.float32).astype(jnp.bfloat16)
```

```python
import functools

import jax
import jax.numpy as jnp
from jax import lax
from jax.experimental import pallas as pl
from jax.experimental.pallas import tpu as pltpu
from jax.sharding import PartitionSpec as P

HEADS = 6
HD = 128
HH = 16
WW = 16
WIN = 8
POOL = 4
TOKENS = HH * WW
PK = (HH // POOL) * (WW // POOL)
HALF = WIN * WW
NEG = -1e30
LOG2E = 1.4426950408889634
MESH = pl.DeviceIdType.MESH
NT = (((1,), (1,)), ((), ()))


def kernel(n, snake, near_reach, ft, gain, x_hbm, wq_hbm, wk_hbm, wv_hbm, wo_hbm, mixed, wo,
           x_v, wq, wk, wv, normed, q_s, k_s, v_s, far, bias, top_s, acc_s, s_s, p_s,
           x_sem, w_sem, ring_send, ring_recv, sib_send, sib_recv):
    rows = x_v.shape[0]
    count = rows // TOKENS
    own = count * PK
    pieces, keys, tile = far.shape
    parts = pieces // 2
    chips = n // 2
    me = lax.axis_index("tm")
    core = me % 2
    chip = me // 2
    half = chips // 2
    reach = (chips // 2, (chips - 1) // 2)

    def chip_at(pos):
        pos = (pos + chips) % chips
        if not snake:
            return pos
        side = pos // half
        return (1 - side) * (2 * pos) + side * (2 * (chips - 1 - pos) + 1)

    if snake:
        place = (1 - chip % 2) * (chip // 2) + (chip % 2) * (chips - 1 - chip // 2)
    else:
        place = chip
    sibling = chip * 2 + (1 - core)
    step_of = (1, -1)
    neighbour = [[chip_at(place + s * jump) * 2 + core for jump in (1, 2)] for s in step_of]

    def limit(way, piece):
        return reach[way] if piece < parts else reach[1 - way]

    def place_of(way, dist, cross):
        if dist == 0:
            return cross * own
        first = (4 * dist - 2) * own
        if 2 * dist == chips:
            return first + cross * own
        return first + (2 * way + cross) * own

    blocks = x_sem.shape[0]
    size = rows // blocks
    loads = []
    for b in range(blocks):
        part = pl.ds(b * size, size)
        loads.append(pltpu.make_async_copy(x_hbm.at[part], x_v.at[part], x_sem.at[b]))
        loads[-1].start()
    weights = []
    for i, (src, dst) in enumerate(((wk_hbm, wk), (wv_hbm, wv), (wq_hbm, wq), (wo_hbm, wo))):
        weights.append(pltpu.make_async_copy(src, dst, w_sem.at[i]))
        weights[-1].start()

    barrier = pltpu.get_barrier_semaphore()
    for other in (*neighbour[0], *neighbour[1], sibling):
        pl.semaphore_signal(barrier, inc=1, device_id={"tm": other}, device_id_type=MESH)

    sub = 32
    for b in range(blocks):
        loads[b].wait()

        def norm(i, carry, b=b):
            part = pl.ds(pl.multiple_of(b * size + i * sub, sub), sub)
            xf = x_v[part, :].astype(jnp.float32)
            scale = lax.rsqrt(jnp.mean(xf * xf, axis=-1, keepdims=True) + 1e-06)
            normed[part, :] = (xf * scale * gain[...]).astype(jnp.bfloat16)
            return carry

        lax.fori_loop(0, size // sub, norm, 0)

    pr = lax.broadcasted_iota(jnp.int32, (own, rows), 0)
    pc = lax.broadcasted_iota(jnp.int32, (own, rows), 1)
    block_of = (pc // TOKENS) * PK + (pc % TOKENS) // (POOL * WW) * (WW // POOL) + (pc % WW) // POOL
    pool = jnp.where(pr == block_of, 1.0 / (POOL * POOL), 0.0).astype(jnp.bfloat16)

    def ring(way, dist, to, piece):
        return pltpu.make_async_remote_copy(
            src_ref=far.at[piece, pl.ds(place_of(way, dist, 0), own)],
            dst_ref=far.at[piece, pl.ds(place_of(way, to, 0), own)],
            send_sem=ring_send.at[way, to - 1, piece], recv_sem=ring_recv.at[way, to - 1, piece],
            device_id={"tm": neighbour[way][to - dist - 1]}, device_id_type=MESH)

    def across(way, dist, piece):
        return pltpu.make_async_remote_copy(
            src_ref=far.at[piece, pl.ds(place_of(way, dist, 0), own)],
            dst_ref=far.at[piece, pl.ds(place_of(way, dist, 1), own)],
            send_sem=sib_send.at[way, dist, piece], recv_sem=sib_recv.at[way, dist, piece],
            device_id={"tm": sibling}, device_id_type=MESH)

    sends = []
    incoming = {}

    def send(way, dist, piece):
        for to in (dist + 2, dist + 1):
            if dist % 2 == 0 and to <= limit(way, piece):
                copy = ring(way, dist, to, piece)
                copy.start()
                sends.append(copy)

    def share(way, dist, piece):
        copy = across(way, dist, piece)
        copy.start()
        sends.append(copy)
        incoming.setdefault(dist, []).append(copy)

    def relay(dist):
        for piece in range(pieces):
            for way in (0, 1):
                if dist <= limit(way, piece):
                    ring(way, (dist - 1) // 2 * 2, dist, piece).wait_recv()
                    send(way, dist, piece)
                    share(way, dist, piece)

    def settle(dists):
        for dist in dists:
            for copy in incoming.get(dist, ()):
                copy.wait_recv()

    means = jnp.dot(pool, normed[...], preferred_element_type=jnp.float32).astype(jnp.bfloat16)
    for base, weight, w in ((0, weights[0], wk), (parts, weights[1], wv)):
        weight.wait()
        for j in range(parts):
            far[base + j, pl.ds(0, own), :] = jnp.dot(
                means, w[:, pl.ds(j * tile, tile)], preferred_element_type=jnp.float32
            ).astype(jnp.bfloat16)
            if base + j == 0:
                pl.semaphore_wait(barrier, 5)
            for way in (0, 1):
                send(way, 0, base + j)
            share(0, 0, base + j)

    def project(w, out):
        out[...] = jnp.dot(normed[...], w[...], preferred_element_type=jnp.float32).astype(jnp.bfloat16)

    project(wk, k_s)
    project(wv, v_s)

    slot = lax.broadcasted_iota(jnp.int32, (1, keys), 1) // PK
    key_time = jnp.zeros((1, keys), jnp.int32)
    for dist in range(reach[0] + 1):
        for way in (0, 1):
            if (dist == 0 or 2 * dist == chips) and way == 1:
                continue
            for cross in (0, 1):
                plane = core * (1 - cross) + (1 - core) * cross
                dev = chip_at(place - step_of[way] * dist) * 2 + plane
                first = place_of(way, dist, cross) // PK
                for f in range(count):
                    key_time = jnp.where(slot == first + f, ft[dev * count + f], key_time)
    for f in range(count):
        bias[f] = jnp.where(key_time < ft[me * count + f], 0.0, NEG)

    weights[2].wait()
    project(wq, q_s)

    ir = lax.broadcasted_iota(jnp.int32, (HALF, HALF), 0)
    ic = lax.broadcasted_iota(jnp.int32, (HALF, HALF), 1)
    near_bias = jnp.where((ir // WIN) % 2 == (ic // WIN) % 2, 0.0, NEG)
    rate = LOG2E / HD**0.5
    cut = min(keys, (4 * near_reach + 2) * own)
    groups = tile // HD

    ones = jnp.ones((1, HD), jnp.bfloat16)

    def with_ones(v):
        return jnp.concatenate([v, jnp.broadcast_to(ones, v.shape)], axis=1)

    def attend(h, lo, size, first, last):
        cols = pl.ds(pl.multiple_of(h * HD, HD), HD)
        inner = pl.ds(pl.multiple_of(h % groups * HD, HD), HD)
        span = pl.ds(0, size)
        k_far = far[h // groups, pl.ds(lo, size), inner]
        v_far = far[parts + h // groups, pl.ds(lo, size), inner]
        s_s[:, span] = lax.dot_general(q_s[:, cols], k_far, NT, preferred_element_type=jnp.float32)
        near = []
        keeps = []
        for block in range(rows // HALF):
            here = pl.ds(block * HALF, HALF)
            s = s_s[here, span] + bias[block * HALF // TOKENS, :, pl.ds(lo, size)]
            if first:
                s0 = lax.dot_general(q_s[here, cols], k_s[here, cols], NT, preferred_element_type=jnp.float32)
                s = jnp.concatenate([s0 + near_bias, s], axis=1)
            top = jnp.broadcast_to(jnp.max(s, -1, keepdims=True), (HALF, HD))
            if not first:
                old = top_s[h, here, :]
                top = jnp.maximum(old, top)
                keeps.append(jnp.exp2((old - top) * rate))
            if not last:
                top_s[h, here, :] = top
            w = jnp.exp2((s - jnp.tile(top, (1, -(-s.shape[1] // HD)))[:, :s.shape[1]]) * rate).astype(jnp.bfloat16)
            if first:
                near.append(jnp.dot(w[:, :HD], with_ones(v_s[here, cols]), preferred_element_type=jnp.float32))
                w = w[:, HD:]
            p_s[here, span] = w
        acc = jnp.dot(p_s[:, span], with_ones(v_far), preferred_element_type=jnp.float32)
        for block in range(rows // HALF):
            here = pl.ds(block * HALF, HALF)
            mine = acc[block * HALF:(block + 1) * HALF]
            if first:
                mine = mine + near[block]
            else:
                mine = mine + acc_s[h, here, :] * jnp.tile(keeps[block], (1, 2))
            if last:
                mixed[here, cols] = (mine[:, :HD] / mine[:, HD:]).astype(jnp.bfloat16)
            else:
                acc_s[h, here, :] = mine

    def first_pass(h, carry):
        attend(h, 0, cut, True, cut == keys)
        return carry

    def second_pass(h, carry):
        attend(h, cut, keys - cut, False, True)
        return carry

    for dist in range(1, near_reach + 1):
        relay(dist)
    settle(range(near_reach + 1))
    later = list(range(near_reach + 1, reach[0] + 1))
    spread = HEADS // 2
    lax.fori_loop(0, spread, first_pass, 0)
    for dist in later[:1]:
        relay(dist)
    lax.fori_loop(spread, HEADS, first_pass, 0)
    for dist in later[1:]:
        relay(dist)
    settle(later)
    if cut < keys:
        lax.fori_loop(0, HEADS, second_pass, 0)
    for copy in sends:
        copy.wait_send()
    weights[3].wait()


def finish(mixed, wo, out_hbm, out_v, sem):
    chunks, rows, width = out_v.shape
    copies = []
    for c in range(chunks):
        cols = pl.ds(c * width, width)
        out_v[c] = jnp.dot(mixed[...], wo[:, cols], preferred_element_type=jnp.float32).astype(jnp.bfloat16)
        copies.append(pltpu.make_async_copy(out_v.at[c], out_hbm.at[:, cols], sem.at[c]))
        copies[-1].start()
    for copy in copies:
        copy.wait()


def on_device(n, snake, frames_in, frame_time, norm_gain, w_query, w_key, w_value, w_output):
    rows, width = frames_in.shape
    inner = w_query.shape[1]
    count = rows // TOKENS
    keys = n * count * PK
    hops = n // 4 + 1
    tile = 2 * HD
    pieces = 2 * (inner // tile)
    near_reach = n // 8
    bf = jnp.bfloat16
    f32 = jnp.float32
    dma = pltpu.SemaphoreType.DMA
    hbm = pl.BlockSpec(memory_space=pl.ANY)
    vmem = pl.BlockSpec(memory_space=pltpu.VMEM)
    mixed, wo = pl.pallas_call(
        functools.partial(kernel, n, snake, near_reach),
        out_shape=(pltpu.VMEM((rows, inner), bf), pltpu.VMEM((inner, width), bf)),
        in_specs=[pl.BlockSpec(memory_space=pltpu.SMEM), vmem, hbm, hbm, hbm, hbm, hbm],
        out_specs=(vmem, vmem),
        scratch_shapes=[
            pltpu.VMEM((rows, width), bf),
            pltpu.VMEM((width, inner), bf),
            pltpu.VMEM((width, inner), bf),
            pltpu.VMEM((width, inner), bf),
            pltpu.VMEM((rows, width), bf),
            pltpu.VMEM((rows, inner), bf),
            pltpu.VMEM((rows, inner), bf),
            pltpu.VMEM((rows, inner), bf),
            pltpu.VMEM((pieces, keys, tile), bf),
            pltpu.VMEM((count, 1, keys), f32),
            pltpu.VMEM((HEADS, rows, HD), f32),
            pltpu.VMEM((HEADS, rows, 2 * HD), f32),
            pltpu.VMEM((rows, keys), f32),
            pltpu.VMEM((rows, keys), bf),
            dma((4,)),
            dma((4,)),
            dma((2, hops, pieces)),
            dma((2, hops, pieces)),
            dma((2, hops, pieces)),
            dma((2, hops, pieces)),
        ],
        compiler_params=pltpu.CompilerParams(
            collective_id=0, has_side_effects=True, vmem_limit_bytes=60 << 20
        ),
    )(frame_time, norm_gain, frames_in, w_query, w_key, w_value, w_output)
    chunks = width // (4 * HD)
    return pl.pallas_call(
        finish,
        out_shape=jax.ShapeDtypeStruct((rows, width), bf),
        in_specs=[vmem, vmem],
        out_specs=hbm,
        scratch_shapes=[pltpu.VMEM((chunks, rows, width // chunks), bf), dma((chunks,))],
        compiler_params=pltpu.CompilerParams(vmem_limit_bytes=8 << 20),
    )(mixed, wo)


def is_snake(mesh):
    names = list(mesh.axis_names)
    line = mesh.devices.transpose(names.index("grp"), names.index("tm"))[0]
    try:
        second = {d.coords[1] for d in line}
        third = {d.coords[2] for d in line}
    except (AttributeError, TypeError):
        return False
    return len(second) == 2 and len(third) * 4 == len(line)


def solution(mesh):
    placed = (P(("grp", "tm"), None), P("grp"), P(), P(), P(), P(), P())
    n = mesh.shape["tm"]
    return jax.shard_map(
        functools.partial(on_device, n, is_snake(mesh)),
        mesh=mesh, in_specs=placed, out_specs=P(("grp", "tm"), None), check_vma=False,
    )
```

```python
import functools

import jax
import jax.numpy as jnp
from jax import lax
from jax.experimental import pallas as pl
from jax.experimental.pallas import tpu as pltpu
from jax.sharding import PartitionSpec as P

HEADS = 6
HD = 128
HH = 16
WW = 16
WIN = 8
POOL = 4
TOKENS = HH * WW
PK = (HH // POOL) * (WW // POOL)
HALF = WIN * WW
NEG = -1e30
LOG2E = 1.4426950408889634
MESH = pl.DeviceIdType.MESH
NT = (((1,), (1,)), ((), ()))


def kernel(n, snake, cut, ft_hbm, gain_hbm, x_hbm, wq_hbm, wk_hbm, wv_hbm, wo_hbm, mixed, wo,
           ft, gain, x_v, wq, wk, wv, normed, q_s, k_s, v_s, far, bias, top_s, acc_s, s_s, p_all,
           x_sem, w_sem, small_sem, send_sem, recv_sem, sib_send, sib_recv):
    rows = x_v.shape[0]
    count = rows // TOKENS
    own = count * PK
    keys = far.shape[1]
    chips = n // 2
    me = lax.axis_index("tm")
    core = me % 2
    chip = me // 2
    sibling = chip * 2 + (1 - core)

    blocks = x_sem.shape[0]
    size = rows // blocks
    loads = []
    for b in range(blocks):
        part = pl.ds(b * size, size)
        loads.append(pltpu.make_async_copy(x_hbm.at[part], x_v.at[part], x_sem.at[b]))
        loads[-1].start()
    small = [pltpu.make_async_copy(gain_hbm, gain, small_sem.at[0]), pltpu.make_async_copy(ft_hbm, ft, small_sem.at[1])]
    for copy in small:
        copy.start()
    weights = []
    for i, (src, dst) in enumerate(((wk_hbm, wk), (wv_hbm, wv), (wq_hbm, wq), (wo_hbm, wo))):
        weights.append(pltpu.make_async_copy(src, dst, w_sem.at[i]))
    for copy in weights:
        copy.start()

    plan = (grid_plan if snake else ring_plan)(n, own, cut, core, chip)
    place_of, peers, slots, hop = plan
    barrier = pltpu.get_barrier_semaphore()
    for other in (*peers, sibling):
        pl.semaphore_signal(barrier, inc=1, device_id={"tm": other}, device_id_type=MESH)

    small[0].wait()
    sub = 32
    for b in range(blocks):
        loads[b].wait()

        def norm(i, carry, b=b):
            part = pl.ds(pl.multiple_of(b * size + i * sub, sub), sub)
            xf = x_v[part, :].astype(jnp.float32)
            scale = lax.rsqrt(jnp.mean(xf * xf, axis=-1, keepdims=True) + 1e-06)
            normed[part, :] = (xf * scale * gain[...]).astype(jnp.bfloat16)
            return carry

        lax.fori_loop(0, size // sub, norm, 0)

    pr = lax.broadcasted_iota(jnp.int32, (own, rows), 0)
    pc = lax.broadcasted_iota(jnp.int32, (own, rows), 1)
    block_of = (pc // TOKENS) * PK + (pc % TOKENS) // (POOL * WW) * (WW // POOL) + (pc % WW) // POOL
    pool = jnp.where(pr == block_of, 1.0 / (POOL * POOL), 0.0).astype(jnp.bfloat16)

    sends = []

    def go(copy):
        copy.start()
        sends.append(copy)

    def remote(piece, name):
        src, dst, device, index = hop(name, piece)
        return pltpu.make_async_remote_copy(
            src_ref=far.at[piece, pl.ds(src, own)], dst_ref=far.at[piece, pl.ds(dst, own)],
            send_sem=send_sem.at[piece, index], recv_sem=recv_sem.at[piece, index],
            device_id={"tm": device}, device_id_type=MESH)

    def across(piece, slot):
        return pltpu.make_async_remote_copy(
            src_ref=far.at[piece, pl.ds(place_of(slot, 0), own)], dst_ref=far.at[piece, pl.ds(place_of(slot, 1), own)],
            send_sem=sib_send.at[piece, place_of(slot, 0) // (2 * own)], recv_sem=sib_recv.at[piece, place_of(slot, 0) // (2 * own)],
            device_id={"tm": sibling}, device_id_type=MESH)

    def first_sends(piece):
        for name in first_hops(piece):
            go(remote(piece, name))
        go(across(piece, slots[0][0]))

    def take(piece, name, slot, onward):
        remote(piece, name).wait_recv()
        for other in onward:
            go(remote(piece, other))
        go(across(piece, slot))

    def settle(piece, wanted):
        for slot, _ in slots:
            if (place_of(slot, 0) < cut) == wanted:
                across(piece, slot).wait_recv()

    first_hops, steps = (grid_steps if snake else ring_steps)(n, cut, own, place_of)

    def advance(*names):
        for name in names:
            for step in steps.get(name, ()):
                take(*step)

    means = jnp.dot(pool, normed[...], preferred_element_type=jnp.float32).astype(jnp.bfloat16)
    for piece, weight, w in ((0, weights[0], wk), (1, weights[1], wv)):
        weight.wait()
        far[piece, pl.ds(0, own), :] = jnp.dot(
            means, w[...], preferred_element_type=jnp.float32
        ).astype(jnp.bfloat16)
        if piece == 0:
            pl.semaphore_wait(barrier, len(peers) + 1)
        first_sends(piece)

    def project(w, out):
        out[...] = jnp.dot(normed[...], w[...], preferred_element_type=jnp.float32).astype(jnp.bfloat16)

    project(wk, k_s)
    project(wv, v_s)
    advance(0)
    weights[2].wait()
    project(wq, q_s)
    advance(1)

    small[1].wait()
    slot = lax.broadcasted_iota(jnp.int32, (1, keys), 1) // PK
    key_time = jnp.zeros((1, keys), jnp.int32)
    for name, source in slots:
        for cross in (0, 1):
            plane = core * (1 - cross) + (1 - core) * cross
            dev = source * 2 + plane
            first = place_of(name, cross) // PK
            for f in range(count):
                key_time = jnp.where(slot == first + f, ft[dev * count + f], key_time)
    for f in range(count):
        bias[f] = jnp.where(key_time < ft[me * count + f], 0.0, NEG)

    ir = lax.broadcasted_iota(jnp.int32, (HALF, HALF), 0)
    ic = lax.broadcasted_iota(jnp.int32, (HALF, HALF), 1)
    near_bias = jnp.where((ir // WIN) % 2 == (ic // WIN) % 2, 0.0, NEG)
    rate = LOG2E / HD**0.5
    rest = keys - cut
    ones = jnp.ones((1, HD), jnp.bfloat16)

    def with_ones(v):
        return jnp.concatenate([v, jnp.broadcast_to(ones, v.shape)], axis=1)

    def near_pass(first, count):
        jobs = [(h, block) for h in range(first, first + count) for block in range(rows // HALF)]
        scores = {}
        for h, block in jobs:
            here, cols = pl.ds(block * HALF, HALF), pl.ds(h * HD, HD)
            scores[h, block] = lax.dot_general(q_s[here, cols], k_s[here, cols], NT, preferred_element_type=jnp.float32)
        for h, block in jobs:
            here, cols = pl.ds(block * HALF, HALF), pl.ds(h * HD, HD)
            s = scores[h, block] + near_bias
            top = jnp.broadcast_to(jnp.max(s, -1, keepdims=True), (HALF, HD))
            top_s[h, here, :] = top
            w = jnp.exp2((s - top) * rate).astype(jnp.bfloat16)
            acc_s[h, here, :] = jnp.dot(w, with_ones(v_s[here, cols]), preferred_element_type=jnp.float32)

    def score(lo, size):
        span = pl.ds(lo, size)

        def body(h, carry):
            cols = pl.ds(pl.multiple_of(h * HD, HD), HD)
            s_s[:, pl.ds(0, size)] = lax.dot_general(q_s[:, cols], far[0, span, cols], NT, preferred_element_type=jnp.float32)
            for block in range(rows // HALF):
                here = pl.ds(block * HALF, HALF)
                s = s_s[here, pl.ds(0, size)] + bias[block * HALF // TOKENS, :, span]
                old = top_s[h, here, :]
                top = jnp.maximum(old, jnp.broadcast_to(jnp.max(s, -1, keepdims=True), (HALF, HD)))
                keep = jnp.exp2((old - top) * rate)
                acc_s[h, here, :] = acc_s[h, here, :] * jnp.tile(keep, (1, 2))
                if lo == 0:
                    top_s[h, here, :] = top
                w = jnp.exp2((s - jnp.tile(top, (1, -(-size // HD)))[:, :size]) * rate)
                p_all[h, here, span] = w.astype(jnp.bfloat16)
            return carry

        return body

    def sum_first(h, carry):
        cols = pl.ds(pl.multiple_of(h * HD, HD), HD)
        span = pl.ds(0, cut)
        acc = jnp.dot(p_all[h, :, span], with_ones(far[1, span, cols]), preferred_element_type=jnp.float32)
        acc_s[h] = acc_s[h] + acc
        return carry

    def sum_rest(h, carry):
        cols = pl.ds(pl.multiple_of(h * HD, HD), HD)
        span = pl.ds(cut, rest)
        acc = jnp.dot(p_all[h, :, span], with_ones(far[1, span, cols]), preferred_element_type=jnp.float32)
        acc = acc + acc_s[h]
        mixed[:, cols] = (acc[:, :HD] / acc[:, HD:]).astype(jnp.bfloat16)
        return carry

    def over(body, name, parts):
        for part in range(parts):
            lax.fori_loop(part * HEADS // parts, (part + 1) * HEADS // parts, body, 0)
            advance(name + part)

    half = HEADS // 2
    for part in range(2):
        near_pass(part * half, half)
        advance(2 + part)
    settle(0, True)
    over(score(0, cut), 4, 3)
    settle(1, True)
    lax.fori_loop(0, HEADS, sum_first, 0)
    advance(7)
    settle(0, False)
    over(score(cut, rest), 8, 2)
    settle(1, False)
    lax.fori_loop(0, HEADS, sum_rest, 0)
    for copy in sends:
        copy.wait_send()
    weights[3].wait()


def flip(z, k):
    out = z
    bit = 1
    while bit <= k:
        if k // bit % 2:
            out = out + bit - 2 * bit * (z // bit % 2)
        bit *= 2
    return out


def grid_plan(n, own, cut, core, chip):
    deep = n // 4
    y = chip % 2
    z = chip // 2

    def place_of(slot, cross):
        k, f = slot
        return (4 * k + 2 * f + cross) * own

    def device(k, f):
        side = y if f == 0 else 1 - y
        return (flip(z, k) * 2 + side) * 2 + core

    def hop(name, piece):
        kind, k = name
        if kind == "z":
            return place_of((0, 0), 0), place_of((k, 0), 0), device(k, 0), k
        return place_of((k, 0), 0), place_of((k, 1), 0), device(0, 1), deep + k

    peers = [device(k, 0) for k in range(1, deep)] + [device(0, 1)]
    slots = [((k, f), device(k, f) // 2) for k in range(deep) for f in (0, 1)]
    return place_of, peers, slots, hop


def grid_steps(n, cut, own, place_of):
    deep = n // 4
    inner = [k for k in range(1, deep) if place_of((k, 0), 0) < cut]
    outer = [k for k in range(1, deep) if place_of((k, 0), 0) >= cut]

    def first_hops(piece):
        return [("z", k) for k in range(1, deep)] + [("y", 0)]

    def from_z(piece, ks):
        return [(piece, ("z", k), (k, 0), [("y", k)]) for k in ks]

    def from_y(piece, ks):
        return [(piece, ("y", k), (k, 1), []) for k in ks]

    steps = {
        0: from_z(0, inner) + from_y(0, [0]),
        1: from_z(1, inner) + from_y(1, [0]),
        2: from_z(0, outer[:1]),
        3: from_z(0, outer[1:]) + from_y(0, inner),
        4: from_z(1, outer[:1]),
        5: from_y(1, inner),
        6: from_z(1, outer[1:]),
        7: from_y(0, outer),
        9: from_y(1, outer),
    }
    return first_hops, steps


def ring_plan(n, own, cut, core, chip):
    chips = n // 2

    def place_of(slot, cross):
        way, dist = slot
        if dist == 0:
            return cross * own
        first = (4 * dist - 2) * own
        if 2 * dist == chips:
            return first + cross * own
        return first + (2 * way + cross) * own

    def chip_at(way, dist):
        return (chip + (1, -1)[way] * dist + chips) % chips

    def hop(name, piece):
        way, dist = name
        return place_of((way, dist - 1), 0), place_of((way, dist), 0), chip_at(way, 1) * 2 + core, way * (chips // 2) + dist - 1

    peers = [chip_at(way, 1) * 2 + core for way in (0, 1)]
    slots = [((0, 0), chip)]
    for dist in range(1, chips // 2 + 1):
        for way in (0, 1) if 2 * dist < chips else (0,):
            slots.append(((way, dist), chip_at(1 - way, dist)))
    return place_of, peers, slots, hop


def ring_steps(n, cut, own, place_of):
    chips = n // 2
    reach = (chips // 2, (chips - 1) // 2)

    def limit(way, piece):
        return reach[way] if piece == 0 else reach[1 - way]

    def first_hops(piece):
        return [(way, 1) for way in (0, 1) if limit(way, piece) >= 1]

    steps = {3: [], 7: []}
    for dist in range(1, reach[0] + 1):
        early = place_of((0, dist), 0) < cut
        for piece in (0, 1):
            name = 3 if early else 7
            for way in (0, 1):
                if dist <= limit(way, piece):
                    onward = [(way, dist + 1)] if dist < limit(way, piece) else []
                    slot = (0, dist) if 2 * dist == chips else (way, dist)
                    steps[name].append((piece, (way, dist), slot, onward))
    return first_hops, steps


def finish(mixed, wo, out_hbm, out_v, sem):
    chunks, rows, width = out_v.shape
    copies = []
    for c in range(chunks):
        cols = pl.ds(c * width, width)
        out_v[c] = jnp.dot(mixed[...], wo[:, cols], preferred_element_type=jnp.float32).astype(jnp.bfloat16)
        copies.append(pltpu.make_async_copy(out_v.at[c], out_hbm.at[:, cols], sem.at[c]))
        copies[-1].start()
    for copy in copies:
        copy.wait()


def on_device(n, snake, frames_in, frame_time, norm_gain, w_query, w_key, w_value, w_output):
    rows, width = frames_in.shape
    inner = w_query.shape[1]
    count = rows // TOKENS
    keys = n * count * PK
    slots = n // 2
    half = keys // 2
    cut = half if snake else half + 2 * count * PK
    bf = jnp.bfloat16
    f32 = jnp.float32
    dma = pltpu.SemaphoreType.DMA
    hbm = pl.BlockSpec(memory_space=pl.ANY)
    vmem = pl.BlockSpec(memory_space=pltpu.VMEM)
    mixed, wo = pl.pallas_call(
        functools.partial(kernel, n, snake, cut),
        out_shape=(pltpu.VMEM((rows, inner), bf), pltpu.VMEM((inner, width), bf)),
        in_specs=[hbm, hbm, hbm, hbm, hbm, hbm, hbm],
        out_specs=(vmem, vmem),
        scratch_shapes=[
            pltpu.SMEM(frame_time.shape, jnp.int32),
            pltpu.VMEM(norm_gain.shape, f32),
            pltpu.VMEM((rows, width), bf),
            pltpu.VMEM((width, inner), bf),
            pltpu.VMEM((width, inner), bf),
            pltpu.VMEM((width, inner), bf),
            pltpu.VMEM((rows, width), bf),
            pltpu.VMEM((rows, inner), bf),
            pltpu.VMEM((rows, inner), bf),
            pltpu.VMEM((rows, inner), bf),
            pltpu.VMEM((2, keys, inner), bf),
            pltpu.VMEM((count, 1, keys), f32),
            pltpu.VMEM((HEADS, rows, HD), f32),
            pltpu.VMEM((HEADS, rows, 2 * HD), f32),
            pltpu.VMEM((rows, cut), f32),
            pltpu.VMEM((HEADS, rows, keys), bf),
            dma((4,)),
            dma((4,)),
            dma((2,)),
            dma((2, slots)),
            dma((2, slots)),
            dma((2, slots)),
            dma((2, slots)),
        ],
        compiler_params=pltpu.CompilerParams(
            collective_id=0, has_side_effects=True, vmem_limit_bytes=60 << 20
        ),
    )(frame_time, norm_gain, frames_in, w_query, w_key, w_value, w_output)
    chunks = width // (4 * HD)
    return pl.pallas_call(
        finish,
        out_shape=jax.ShapeDtypeStruct((rows, width), bf),
        in_specs=[vmem, vmem],
        out_specs=hbm,
        scratch_shapes=[pltpu.VMEM((chunks, rows, width // chunks), bf), dma((chunks,))],
        compiler_params=pltpu.CompilerParams(vmem_limit_bytes=8 << 20),
    )(mixed, wo)


def is_snake(mesh):
    names = list(mesh.axis_names)
    line = mesh.devices.transpose(names.index("grp"), names.index("tm"))[0]
    try:
        second = {d.coords[1] for d in line}
        third = {d.coords[2] for d in line}
    except (AttributeError, TypeError):
        return False
    deep = len(third)
    return len(second) == 2 and deep * 4 == len(line) and deep in [2**k for k in range(deep)]


def solution(mesh):
    placed = (P(("grp", "tm"), None), P("grp"), P(), P(), P(), P(), P())
    n = mesh.shape["tm"]
    return jax.shard_map(
        functools.partial(on_device, n, is_snake(mesh)),
        mesh=mesh, in_specs=placed, out_specs=P(("grp", "tm"), None), check_vma=False,
    )
```
